32 devices in a mesh: blk: 4 (over z), sub: 8 (over y, x, core).
Axes of the slice: x: 2, y: 2, z: 4, core: 2. Of those that a mesh axis runs over, the one named last changes fastest.
Arguments:
- fields: float32 [32, 55, 2197], P(('blk', 'sub')), may hold values from -6 to 6
- flux_matrix: float32 [3, 55, 55], replicated, may hold values from -0.875 to 0.875
- inv_jacobian: float32 [32, 3], P(('blk', 'sub')), may hold values from 1 to 4
- neighbour: int32 [32, 6], P(('blk', 'sub')), may hold values from 0 to 31, as said below
- orientation: int32 [32, 6], P(('blk', 'sub')), may hold values from 0 to 7, as said below
- face_order: int32 [32, 6], P(('blk', 'sub')), may hold values from 9 to 13, as said below
Outputs:
- increment: float32 [32, 55, 2197], P(('blk', 'sub'))
The draws below stay inside these ranges and needn't reach their ends.
Inputs may be any that keep to these rules, and one draw needn't show every extreme that they name: Element g belongs to the device with blk index (g) // 8 and sub index (g) % 8. The neighbour across face 0 (face 1) lies on the device one step lower (higher) along blk, cyclically, with the same sub index; across face 2 (face 3) on the device one step lower (higher) along sub, cyclically, with the same blk index; across faces 4 and 5 on the same device. If h = neighbour[g, f] then neighbour[h, f xor 1] = g, and the faces of one direction pair the elements of two devices one to one. `orientation`: the two sides of a face carry mutually inverse codes under orient. `face_order`: the two sides of a face carry the same order.
All inputs are finite; a program needn't handle non-finite values.
Results may differ from the reference program's by a relative error of at most 0.002.
Values may be sent and summed in bfloat16 or wider, within the bound.
A program may use at most 64 MiB of HBM per device.

```python
import math
import jax
import jax.numpy as jnp
from jax import lax

VARS = 55
PTS = 13
LOW_ORDER = 9
E_DEV = 1
ELEMS = 32
N_BLK = 4
N_SUB = 8


def invert_code(face_code):
    turned = 4 + 2 * (face_code % 2) + face_code // 2 % 2
    return jnp.where(face_code >= 4, turned, face_code)


def mesh_tables(key):
    device_count = N_BLK * N_SUB
    column_len = E_DEV
    base_key = jax.random.fold_in(key, 7)
    key_perm, key_code, key_order = jax.random.split(base_key, 3)
    scores = jax.random.randint(key_perm, (device_count, column_len), 0, 1 << 20) * column_len + jnp.arange(column_len, dtype=jnp.int32)[None, :]
    column = jnp.argsort(scores, axis=1).astype(jnp.int32)
    position = jnp.argsort(column, axis=1).astype(jnp.int32)
    plus_code = jax.random.randint(key_code, (device_count, column_len, 3), 0, 8).astype(jnp.int32)
    plus_order = jax.random.randint(key_order, (device_count, column_len, 3), LOW_ORDER, PTS + 1).astype(jnp.int32)
    shape_two = (device_count, column_len)
    device_id = jnp.broadcast_to(jnp.arange(device_count, dtype=jnp.int32)[:, None], shape_two)
    slot_pos = jnp.broadcast_to(jnp.arange(column_len, dtype=jnp.int32)[None, :], shape_two)
    row_id = device_id // N_SUB
    col_id = device_id % N_SUB
    down_x = (row_id - 1) % N_BLK * N_SUB + col_id
    up_x = (row_id + 1) % N_BLK * N_SUB + col_id
    down_y = row_id * N_SUB + (col_id - 1) % N_SUB
    up_y = row_id * N_SUB + (col_id + 1) % N_SUB
    down_z = (slot_pos - 1) % column_len
    up_z = (slot_pos + 1) % column_len
    nb_device = jnp.stack([down_x, up_x, down_y, up_y, device_id, device_id], axis=-1)
    nb_slot = jnp.stack([slot_pos, slot_pos, slot_pos, slot_pos, down_z, up_z], axis=-1)
    ids = nb_device * column_len + column[nb_device, nb_slot]
    codes = jnp.stack([invert_code(plus_code[down_x, slot_pos, 0]), plus_code[device_id, slot_pos, 0], invert_code(plus_code[down_y, slot_pos, 1]), plus_code[device_id, slot_pos, 1], invert_code(plus_code[device_id, down_z, 2]), plus_code[device_id, slot_pos, 2]], axis=-1)
    orders = jnp.stack([plus_order[down_x, slot_pos, 0], plus_order[device_id, slot_pos, 0], plus_order[down_y, slot_pos, 1], plus_order[device_id, slot_pos, 1], plus_order[device_id, down_z, 2], plus_order[device_id, slot_pos, 2]], axis=-1)
    pick = position[:, :, None]
    ids = jnp.take_along_axis(ids, pick, axis=1).reshape(device_count * column_len, 6)
    codes = jnp.take_along_axis(codes, pick, axis=1).reshape(device_count * column_len, 6)
    orders = jnp.take_along_axis(orders, pick, axis=1).reshape(device_count * column_len, 6)
    return (ids.astype(jnp.int32), codes.astype(jnp.int32), orders.astype(jnp.int32))


def draw_neighbour(key, part):
    return mesh_tables(key)[0]


def draw_orientation(key, part):
    return mesh_tables(key)[1]


def draw_face_order(key, part):
    return mesh_tables(key)[2]


def steps_of(own_key, shape, cuts, low, largest):
    level = 1.0
    for dim, parts in cuts:
        heights = jax.random.uniform(jax.random.fold_in(jax.random.fold_in(own_key, 6), dim), (parts,), jnp.float32, low / len(cuts), largest / len(cuts))
        level = level * jnp.repeat(jnp.exp(heights), shape[dim] // parts).reshape((-1,) + (1,) * (len(shape) - 1 - dim))
    return level


def gaussian(stream_key, extent, deviation, bound, cuts=(), held_as=jnp.bfloat16):
    loudness = steps_of(stream_key, extent, cuts, -0.22, 0.18) if cuts else 1.0
    values = jax.random.normal(stream_key, extent, jnp.float32) * deviation * loudness
    return jnp.minimum(jnp.maximum(values, -bound), bound).astype(held_as)


def setup_inputs(seed: int = 0) -> dict:
    key_of = jax.random.split(jax.random.key(seed), 7)
    return {
        "fields": gaussian(key_of[0], (ELEMS, VARS, PTS ** 3), 1.0, 6.0, ((0, 32),), jnp.float32),
        "flux_matrix": gaussian(key_of[1], (3, VARS, VARS), VARS ** -0.5, 0.875, (), jnp.float32),
        "inv_jacobian": jnp.clip(jnp.exp(math.log(4.0) - 1.3862944 * jax.random.uniform(key_of[2], (ELEMS, 3), jnp.float32) ** steps_of(key_of[2], (ELEMS, 3), ((0, 32),), -0.2, 0.2)), 1.0, 4.0),
        "neighbour": draw_neighbour(jax.random.fold_in(key_of[6], 71), 0),
        "orientation": draw_orientation(jax.random.fold_in(key_of[6], 71), 0),
        "face_order": draw_face_order(jax.random.fold_in(key_of[6], 71), 0),
    }


penalty = 1.0
time_step = 0.01
highest = lax.Precision.HIGHEST

def cheb_matrix(point_count):
    last_node = point_count - 1
    node_index = jnp.arange(point_count, dtype=jnp.int32)
    node_values = -jnp.cos(jnp.pi * node_index.astype(jnp.float32) / last_node)
    weights = jnp.where((node_index == 0) | (node_index == last_node), 2.0, 1.0) * jnp.where(node_index % 2 == 0, 1.0, -1.0)
    weights = weights.astype(jnp.float32)
    identity = jnp.eye(point_count, dtype=jnp.float32)
    node_gap = node_values[:, None] - node_values[None, :] + identity
    off_diag = weights[:, None] / weights[None, :] / node_gap * (1.0 - identity)
    return off_diag - jnp.diag(lax.optimization_barrier(jnp.sum(off_diag, axis=1)))

def dct_matrix(point_count):
    row_index = jnp.arange(point_count, dtype=jnp.float32)[:, None]
    col_index = jnp.arange(point_count, dtype=jnp.float32)[None, :]
    dct_basis = jnp.cos(jnp.pi * row_index * (col_index + 0.5) / point_count) * jnp.sqrt(2.0 / point_count)
    return dct_basis * jnp.where(row_index == 0, jnp.sqrt(0.5), 1.0).astype(jnp.float32)

def orient_face(face_trace, face_code):
    shaped = face_code[:, None, None, None]
    flipped = jnp.where(shaped // 2 % 2 == 1, jnp.flip(face_trace, 2), face_trace)
    flipped = jnp.where(shaped % 2 == 1, jnp.flip(flipped, 3), flipped)
    return jnp.where(shaped >= 4, jnp.swapaxes(flipped, 2, 3), flipped)

def project(face_trace, mode_order, dct_basis):
    modes = jnp.einsum('ka,fvab,lb->fvkl', dct_basis, face_trace, dct_basis, precision=highest)
    mode_index = jnp.arange(dct_basis.shape[0], dtype=jnp.int32)
    keep = (mode_index[None, :] < mode_order[:, None]).astype(jnp.float32)
    mask_grid = keep[:, None, :, None] * keep[:, None, None, :]
    return jnp.einsum('ka,fvkl,lb->fvab', dct_basis, modes * mask_grid, dct_basis, precision=highest)

def face_jump(own_trace, remote_trace, face_code, mode_order, dct_basis):
    turned = orient_face(remote_trace.astype(jnp.float32), face_code)
    return project(turned, mode_order, dct_basis) - project(own_trace.astype(jnp.float32), mode_order, dct_basis)

def face_traces(element_cube):
    last_index = element_cube.shape[-1] - 1
    return jnp.stack([element_cube[:, :, 0], element_cube[:, :, last_index], element_cube[:, :, :, 0], element_cube[:, :, :, last_index], element_cube[:, :, :, :, 0], element_cube[:, :, :, :, last_index]], axis=1)

def volume_rate(element_cube, flux_matrix, inv_jacobian, derivative):
    along_x = jnp.einsum('ai,evijk->evajk', derivative, element_cube, precision=highest)
    along_y = jnp.einsum('aj,evijk->eviak', derivative, element_cube, precision=highest)
    along_z = jnp.einsum('ak,evijk->evija', derivative, element_cube, precision=highest)
    summed = jnp.zeros(element_cube.shape, jnp.float32)
    for axis_id, along in enumerate((along_x, along_y, along_z)):
        mixed = jnp.einsum('wv,evijk->ewijk', flux_matrix[axis_id], along, precision=highest)
        summed = summed + inv_jacobian[:, axis_id][:, None, None, None, None] * mixed
    return -summed

def add_faces(tendency, corrections, inv_jacobian, lift):
    last_index = tendency.shape[-1] - 1
    scaled = [corrections[face_id] * (lift * inv_jacobian[:, face_id // 2])[:, None, None, None] for face_id in range(6)]
    tendency = tendency.at[:, :, 0].add(scaled[0])
    tendency = tendency.at[:, :, last_index].add(scaled[1])
    tendency = tendency.at[:, :, :, 0].add(scaled[2])
    tendency = tendency.at[:, :, :, last_index].add(scaled[3])
    tendency = tendency.at[:, :, :, :, 0].add(scaled[4])
    tendency = tendency.at[:, :, :, :, last_index].add(scaled[5])
    return tendency

def reference(fields, flux_matrix, inv_jacobian, neighbour, orientation, face_order):
    element_cube = fields.reshape(ELEMS, VARS, PTS, PTS, PTS)
    derivative = cheb_matrix(PTS)
    dct_basis = dct_matrix(PTS)
    traces = face_traces(element_cube).astype(jnp.bfloat16)
    other_face = jnp.array([1, 0, 3, 2, 5, 4], dtype=jnp.int32)
    normal_sign = jnp.array([-1.0, 1.0, -1.0, 1.0, -1.0, 1.0], dtype=jnp.float32)
    face_axis = jnp.array([0, 0, 1, 1, 2, 2], dtype=jnp.int32)
    signed = flux_matrix[face_axis] * normal_sign[:, None, None]
    lift = 0.5 * (PTS - 1) ** 2

    def one_block(first_row):
        block_cube = lax.dynamic_slice_in_dim(element_cube, first_row, E_DEV, 0)
        block_jac = lax.dynamic_slice_in_dim(inv_jacobian, first_row, E_DEV, 0)
        block_neigh = lax.dynamic_slice_in_dim(neighbour, first_row, E_DEV, 0).astype(jnp.int32)
        block_code = lax.dynamic_slice_in_dim(orientation, first_row, E_DEV, 0)
        block_order = lax.dynamic_slice_in_dim(face_order, first_row, E_DEV, 0)
        own_traces = lax.dynamic_slice_in_dim(traces, first_row, E_DEV, 0)
        remote = traces[block_neigh, other_face[None, :]]
        jump_all = face_jump(own_traces.reshape(E_DEV * 6, VARS, PTS, PTS), remote.reshape(E_DEV * 6, VARS, PTS, PTS), block_code.reshape(E_DEV * 6), block_order.reshape(E_DEV * 6), dct_basis).reshape(E_DEV, 6, VARS, PTS, PTS)
        moved_all = jnp.einsum('fwv,efvab->efwab', signed, jump_all, precision=highest)
        corr_all = 0.5 * (penalty * jump_all - moved_all)
        tendency = volume_rate(block_cube, flux_matrix, block_jac, derivative)
        tendency = add_faces(tendency, [corr_all[:, face_id] for face_id in range(6)], block_jac, lift)
        return (time_step * tendency).reshape(E_DEV, VARS, PTS ** 3)
    starts = jnp.arange(ELEMS // E_DEV, dtype=jnp.int32) * E_DEV
    return lax.map(one_block, starts).reshape(ELEMS, VARS, PTS ** 3)
```

```python
import functools

import jax
import jax.numpy as jnp
import numpy as np
from jax import lax
from jax.experimental import pallas as pl
from jax.experimental.pallas import tpu as pltpu
from jax.sharding import PartitionSpec as P

MESH = pl.DeviceIdType.MESH
BF = jnp.bfloat16
F32 = jnp.float32
ROWS = 64
LANES = 256
TIME_STEP = 0.01


def cheb_np(n):
    idx = np.arange(n)
    x = -np.cos(np.pi * idx / (n - 1))
    c = np.where((idx == 0) | (idx == n - 1), 2.0, 1.0) * np.where(idx % 2 == 0, 1.0, -1.0)
    eye = np.eye(n)
    off = c[:, None] / c[None, :] / (x[:, None] - x[None, :] + eye) * (1.0 - eye)
    return off - np.diag(off.sum(axis=1))


def dct_np(n):
    k = np.arange(n)[:, None]
    j = np.arange(n)[None, :]
    basis = np.cos(np.pi * k * (j + 0.5) / n) * np.sqrt(2.0 / n)
    return basis * np.where(k == 0, np.sqrt(0.5), 1.0)


def hi_lo(matrix):
    full = matrix.astype(np.float32)
    hi = full.astype(BF)
    lo = (full - hi.astype(np.float32)).astype(BF)
    return np.stack([hi, lo])


def wide(matrix):
    return np.pad(matrix, ((0, 0), (0, LANES - matrix.shape[1])))


def tables(n):
    plane = n * n
    d = cheb_np(n)
    c = dct_np(n)
    eye = np.eye(n)
    along_y = np.kron(d.T, eye)
    along_z = np.kron(eye, d.T)
    deriv = hi_lo(np.concatenate([wide(along_y), wide(along_z)], axis=1))
    forward = np.kron(c.T, c.T)
    swapped = forward.reshape(plane, n, n).transpose(0, 2, 1).reshape(plane, plane)
    fwd = hi_lo(np.concatenate([wide(forward), wide(swapped)], axis=1))
    back = hi_lo(wide(np.kron(c, c)))
    lane = np.arange(LANES)
    first = np.where(lane < plane, lane // n, 999)
    second = np.where(lane < plane, lane % n, 999)
    ends = lambda v: np.where(v == 0, -1.0, np.where(v == n - 1, 1.0, 0.0))
    sign = lambda v: np.where(v % 2 == 0, 1.0, -1.0)
    lanes = np.stack(
        [first, second, ends(first), ends(second), sign(first), sign(second), first * 0, first * 0]
    ).astype(np.float32)
    return deriv, fwd, back, lanes, d


def body(
    n, diff, sizes,
    code_ref, order_ref, jac_ref, fields_ref, flux_ref, deriv_ref, fwd_ref, back_ref, lane_ref,
    out_ref,
    xf, xs, xl, zs, zl, zyz, zx, own, remote, fc, send_sem, recv_sem,
):
    width = fields_ref.shape[1]
    plane = n * n
    last = n - 1
    blk, sub = lax.axis_index("blk"), lax.axis_index("sub")
    n_blk, n_sub = sizes
    across = [
        (lax.rem(blk + n_blk - 1, n_blk), sub),
        (lax.rem(blk + 1, n_blk), sub),
        (blk, lax.rem(sub + n_sub - 1, n_sub)),
        (blk, lax.rem(sub + 1, n_sub)),
    ]
    barrier = pltpu.get_barrier_semaphore()
    for device in across:
        pl.semaphore_signal(barrier, inc=1, device_id=device, device_id_type=MESH)

    first = lane_ref[0:1, :]
    second = lane_ref[1:2, :]

    for i in range(n):
        slab = fields_ref[0, :, plane * i : plane * (i + 1)]
        slab = jnp.pad(slab, ((0, ROWS - width), (0, LANES - plane)))
        xf[i] = slab
        xs[i] = slab.astype(BF)
        xl[i] = (slab - slab.astype(BF).astype(F32)).astype(BF)
    stack = xs[...].reshape(n * ROWS, LANES)[:, :plane]
    stack_lo = xl[...].reshape(n * ROWS, LANES)[:, :plane]

    own[0] = xs[0]
    own[1] = xs[last]
    row_id = lax.broadcasted_iota(jnp.int32, (plane, LANES), 0).astype(F32)
    starts = [second, second + n * last, second * n, second * n + last]

    def trace(face):
        pick = jnp.where(row_id == starts[face - 2], 1.0, 0.0).astype(BF)
        spread = jnp.dot(stack, pick, preferred_element_type=F32).reshape(n, ROWS, LANES)
        total = jnp.zeros((ROWS, LANES), F32)
        for i in range(n):
            total = jnp.where(first == float(i), spread[i], total)
        own[face] = total.astype(BF)

    trace(2)
    trace(3)
    pl.semaphore_wait(barrier, 4)
    copies = []
    for face in range(4):
        copy = pltpu.make_async_remote_copy(
            src_ref=own.at[face],
            dst_ref=remote.at[face ^ 1],
            send_sem=send_sem.at[face],
            recv_sem=recv_sem.at[face ^ 1],
            device_id=across[face],
            device_id_type=MESH,
        )
        copy.start()
        copies.append(copy)
    trace(4)
    trace(5)

    fc[...] = jnp.zeros_like(fc)
    for axis in range(3):
        scaled = flux_ref[axis] * (-TIME_STEP * jac_ref[0, axis])
        fc[axis, 0:width, 0:width] = scaled
    flux = jnp.concatenate([fc[0], fc[1], fc[2]], axis=1)
    flux_hi = flux.astype(BF)
    flux_lo = (flux - flux_hi.astype(F32)).astype(BF)
    flux_both = jnp.concatenate([flux_hi, flux_lo], axis=0)

    zyz[...] = (
        jnp.dot(stack, deriv_ref[0], preferred_element_type=F32)
        + jnp.dot(stack, deriv_ref[1], preferred_element_type=F32)
        + jnp.dot(stack_lo, deriv_ref[0], preferred_element_type=F32)
    ).reshape(n, ROWS, 2 * LANES)

    for r in range(0, ROWS, 16):
        for c in range(0, LANES, 128):
            parts = [xf[a, r : r + 16, c : c + 128] for a in range(n)]
            for i in range(n):
                total = parts[0] * float(diff[i, 0])
                for a in range(1, n):
                    total = total + parts[a] * float(diff[i, a])
                zx[i, r : r + 16, c : c + 128] = total

    own_flat = own[...].reshape(6 * ROWS, LANES)[:, :plane]
    own_modes = (
        jnp.dot(own_flat, fwd_ref[0, :, :LANES], preferred_element_type=F32)
        + jnp.dot(own_flat, fwd_ref[1, :, :LANES], preferred_element_type=F32)
    ).reshape(6, ROWS, LANES)

    for copy in copies:
        copy.wait()

    far = jnp.concatenate([remote[...], own[5:6], own[4:5]], axis=0)
    far = far.reshape(6 * ROWS, LANES)[:, :plane]
    far_modes = (
        jnp.dot(far, fwd_ref[0], preferred_element_type=F32)
        + jnp.dot(far, fwd_ref[1], preferred_element_type=F32)
    ).reshape(6, ROWS, 2 * LANES)
    ones = jnp.ones((1, LANES), F32)
    sign_first = lane_ref[4:5, :]
    sign_second = lane_ref[5:6, :]
    modes = []
    for face in range(6):
        code = code_ref[0, face]
        order = order_ref[0, face].astype(F32)
        swap = code >= 4
        rev_a = lax.rem(lax.div(code, 2), 2)
        rev_b = lax.rem(code, 2)
        use_first = jnp.where(swap, rev_b, rev_a) == 1
        use_second = jnp.where(swap, rev_a, rev_b) == 1
        sign = jnp.where(use_first, sign_first, ones) * jnp.where(use_second, sign_second, ones)
        keep = jnp.where((first < order) & (second < order), 1.0, 0.0)
        turned = jnp.where(swap, far_modes[face, :, LANES:], far_modes[face, :, :LANES])
        modes.append((turned * sign - own_modes[face]) * keep)
    modes = jnp.concatenate(modes, axis=0)[:, :plane]
    modes_hi = modes.astype(BF)
    modes_lo = (modes - modes_hi.astype(F32)).astype(BF)
    modes = modes_hi
    jump = (
        jnp.dot(modes_lo, back_ref[0], preferred_element_type=F32)
        + jnp.dot(modes, back_ref[0], preferred_element_type=F32)
        + jnp.dot(modes, back_ref[1], preferred_element_type=F32)
    ).reshape(6, ROWS, LANES)
    lift = 0.5 * last * last * 0.5
    jump = jump * lift

    row_int = lax.broadcasted_iota(jnp.int32, (plane, LANES), 0)
    row_second = row_int - n * lax.div(row_int, n)
    col = lax.broadcasted_iota(jnp.int32, (plane, LANES), 1)
    places = [row_second, row_second + n * last, row_second * n, row_second * n + last]
    blocks = [[], [], [], []]
    for f in range(4):
        for i in range(n):
            blocks[f].append(jnp.where(first == float(i), jump[f + 2], 0.0).astype(BF))
    scat = []
    for axis in range(2):
        total = None
        for side in range(2):
            f = 2 * axis + side
            put = jnp.where(col == places[f], 1.0 if side else -1.0, 0.0).astype(BF)
            part = jnp.dot(
                jnp.concatenate(blocks[f], axis=0)[:, :plane], put, preferred_element_type=F32
            )
            total = part if total is None else total + part
        scat.append(total.reshape(n, ROWS, LANES))

    gain_y = lane_ref[2:3, :] * (TIME_STEP * jac_ref[0, 1])
    gain_z = lane_ref[3:4, :] * (TIME_STEP * jac_ref[0, 2])
    gain_x = TIME_STEP * jac_ref[0, 0]
    zx[0] = zx[0] - jump[0]
    zx[last] = zx[last] + jump[1]

    def keep_both(i, axis, value):
        hi = value.astype(BF)
        zs[i, axis] = hi
        zl[i, axis] = (value - hi.astype(F32)).astype(BF)

    for i in range(n):
        keep_both(i, 0, zx[i])
        keep_both(i, 1, zyz[i, :, :LANES] + scat[0][i])
        keep_both(i, 2, zyz[i, :, LANES:] + scat[1][i])
        both = jnp.dot(
            flux_both, zs[i].reshape(3 * ROWS, LANES), preferred_element_type=F32
        )
        moved = both[:ROWS] + both[ROWS:] + jnp.dot(
            flux_hi, zl[i].reshape(3 * ROWS, LANES), preferred_element_type=F32
        )
        moved = moved + scat[0][i] * gain_y + scat[1][i] * gain_z
        if i == 0:
            moved = moved + jump[0] * gain_x
        if i == last:
            moved = moved + jump[1] * gain_x
        out_ref[0, :, plane * i : plane * (i + 1)] = moved[:width, :plane]


def solution(mesh):
    sizes = (mesh.shape["blk"], mesh.shape["sub"])

    def on_device(fields, flux_matrix, inv_jacobian, neighbour, orientation, face_order):
        points = fields.shape[2]
        n = round(points ** (1.0 / 3.0))
        deriv, fwd, back, lanes, diff = tables(n)
        smem = pl.BlockSpec(memory_space=pltpu.SMEM)
        vmem = pl.BlockSpec(memory_space=pltpu.VMEM)
        return pl.pallas_call(
            functools.partial(body, n, diff, sizes),
            out_shape=jax.ShapeDtypeStruct(fields.shape, F32),
            in_specs=[smem] * 3 + [vmem] * 6,
            out_specs=vmem,
            scratch_shapes=[
                pltpu.VMEM((n, ROWS, LANES), F32),
                pltpu.VMEM((n, ROWS, LANES), BF),
                pltpu.VMEM((n, ROWS, LANES), BF),
                pltpu.VMEM((n, 3, ROWS, LANES), BF),
                pltpu.VMEM((n, 3, ROWS, LANES), BF),
                pltpu.VMEM((n, ROWS, 2 * LANES), F32),
                pltpu.VMEM((n, ROWS, LANES), F32),
                pltpu.VMEM((6, ROWS, LANES), BF),
                pltpu.VMEM((4, ROWS, LANES), BF),
                pltpu.VMEM((3, ROWS, ROWS), F32),
                pltpu.SemaphoreType.DMA((4,)),
                pltpu.SemaphoreType.DMA((4,)),
            ],
            compiler_params=pltpu.CompilerParams(
                collective_id=0, has_side_effects=True, vmem_limit_bytes=48 * 1024 * 1024
            ),
        )(
            orientation, face_order, inv_jacobian, fields, flux_matrix,
            jnp.asarray(deriv), jnp.asarray(fwd), jnp.asarray(back), jnp.asarray(lanes),
        )

    return jax.shard_map(
        on_device,
        mesh=mesh,
        in_specs=(
            P(("blk", "sub"), None, None),
            P(),
            P(("blk", "sub"), None),
            P(("blk", "sub"), None),
            P(("blk", "sub"), None),
            P(("blk", "sub"), None),
        ),
        out_specs=P(("blk", "sub"), None, None),
        check_vma=False,
    )
```

```python
import functools

import jax
import jax.numpy as jnp
import numpy as np
from jax import lax
from jax.experimental import pallas as pl
from jax.experimental.pallas import tpu as pltpu
from jax.sharding import PartitionSpec as P

MESH = pl.DeviceIdType.MESH
BF = jnp.bfloat16
F32 = jnp.float32
ROWS = 64
LANES = 256
TIME_STEP = 0.01


def cheb_np(n):
    idx = np.arange(n)
    x = -np.cos(np.pi * idx / (n - 1))
    c = np.where((idx == 0) | (idx == n - 1), 2.0, 1.0) * np.where(idx % 2 == 0, 1.0, -1.0)
    eye = np.eye(n)
    off = c[:, None] / c[None, :] / (x[:, None] - x[None, :] + eye) * (1.0 - eye)
    return off - np.diag(off.sum(axis=1))


def dct_np(n):
    k = np.arange(n)[:, None]
    j = np.arange(n)[None, :]
    basis = np.cos(np.pi * k * (j + 0.5) / n) * np.sqrt(2.0 / n)
    return basis * np.where(k == 0, np.sqrt(0.5), 1.0)


def hi_lo(matrix):
    full = matrix.astype(np.float32)
    hi = full.astype(BF)
    lo = (full - hi.astype(np.float32)).astype(BF)
    return np.stack([hi, lo])


def wide(matrix):
    return np.pad(matrix, ((0, 0), (0, LANES - matrix.shape[1])))


def tables(n):
    plane = n * n
    d = cheb_np(n)
    c = dct_np(n)
    eye = np.eye(n)
    along_y = np.kron(d.T, eye)
    along_z = np.kron(eye, d.T)
    deriv = hi_lo(np.concatenate([wide(along_y), wide(along_z)], axis=1))
    forward = np.kron(c.T, c.T)
    swapped = forward.reshape(plane, n, n).transpose(0, 2, 1).reshape(plane, plane)
    fwd = hi_lo(np.concatenate([wide(forward), wide(swapped)], axis=1))
    back = hi_lo(wide(np.kron(c, c)))
    lane = np.arange(LANES)
    first = np.where(lane < plane, lane // n, 999)
    second = np.where(lane < plane, lane % n, 999)
    ends = lambda v: np.where(v == 0, -1.0, np.where(v == n - 1, 1.0, 0.0))
    sign = lambda v: np.where(v % 2 == 0, 1.0, -1.0)
    lanes = np.stack(
        [first, second, ends(first), ends(second), sign(first), sign(second), first * 0, first * 0]
    ).astype(np.float32)
    return deriv, fwd, back, lanes, d


def body(
    n, diff, sizes,
    code_ref, order_ref, jac_ref, fields_ref, flux_ref, deriv_ref, fwd_ref, back_ref, lane_ref,
    out_ref,
    xf, xs, xl, zs, zl, zyz, zx, own, remote, fc, send_sem, recv_sem,
):
    width = fields_ref.shape[0]
    plane = n * n
    last = n - 1
    blk, sub = lax.axis_index("blk"), lax.axis_index("sub")
    n_blk, n_sub = sizes
    across = [
        (lax.rem(blk + n_blk - 1, n_blk), sub),
        (lax.rem(blk + 1, n_blk), sub),
        (blk, lax.rem(sub + n_sub - 1, n_sub)),
        (blk, lax.rem(sub + 1, n_sub)),
    ]
    barrier = pltpu.get_barrier_semaphore()
    for device in across:
        pl.semaphore_signal(barrier, inc=1, device_id=device, device_id_type=MESH)

    first = lane_ref[0:1, :]
    second = lane_ref[1:2, :]

    for i in range(n):
        slab = fields_ref[:, 0, plane * i : plane * (i + 1)]
        slab = jnp.pad(slab, ((0, ROWS - width), (0, LANES - plane)))
        xf[i] = slab
        xs[i] = slab.astype(BF)
        xl[i] = (slab - slab.astype(BF).astype(F32)).astype(BF)
    stack = xs[...].reshape(n * ROWS, LANES)[:, :plane]
    stack_lo = xl[...].reshape(n * ROWS, LANES)[:, :plane]

    own[0] = xs[0]
    own[1] = xs[last]
    row_id = lax.broadcasted_iota(jnp.int32, (plane, LANES), 0).astype(F32)
    starts = [second, second + n * last, second * n, second * n + last]

    def trace(face):
        pick = jnp.where(row_id == starts[face - 2], 1.0, 0.0).astype(BF)
        spread = jnp.dot(stack, pick, preferred_element_type=F32).reshape(n, ROWS, LANES)
        total = jnp.zeros((ROWS, LANES), F32)
        for i in range(n):
            total = jnp.where(first == float(i), spread[i], total)
        own[face] = total.astype(BF)

    trace(2)
    trace(3)
    pl.semaphore_wait(barrier, 4)
    copies = []
    for face in range(4):
        copy = pltpu.make_async_remote_copy(
            src_ref=own.at[face],
            dst_ref=remote.at[face ^ 1],
            send_sem=send_sem.at[face],
            recv_sem=recv_sem.at[face ^ 1],
            device_id=across[face],
            device_id_type=MESH,
        )
        copy.start()
        copies.append(copy)
    trace(4)
    trace(5)

    fc[...] = jnp.zeros_like(fc)
    for axis in range(3):
        scaled = flux_ref[axis] * (-TIME_STEP * jac_ref[0, axis])
        fc[axis, 0:width, 0:width] = scaled
    flux = jnp.concatenate([fc[0], fc[1], fc[2]], axis=1)
    flux_hi = flux.astype(BF)
    flux_lo = (flux - flux_hi.astype(F32)).astype(BF)
    flux_both = jnp.concatenate([flux_hi, flux_lo], axis=0)

    zyz[...] = (
        jnp.dot(stack, deriv_ref[0], preferred_element_type=F32)
        + jnp.dot(stack, deriv_ref[1], preferred_element_type=F32)
        + jnp.dot(stack_lo, deriv_ref[0], preferred_element_type=F32)
    ).reshape(n, ROWS, 2 * LANES)

    for r in range(0, ROWS, 16):
        for c in range(0, LANES, 128):
            parts = [xf[a, r : r + 16, c : c + 128] for a in range(n)]
            half = n // 2
            odd = [parts[a] - parts[last - a] for a in range(half)]
            even = [parts[a] + parts[last - a] for a in range(half)]
            for i in range(n - half):
                plus = odd[0] * float(0.5 * (diff[i, 0] - diff[i, last]))
                for a in range(1, half):
                    plus = plus + odd[a] * float(0.5 * (diff[i, a] - diff[i, last - a]))
                if i == last - i:
                    zx[i, r : r + 16, c : c + 128] = plus
                    continue
                minus = even[0] * float(0.5 * (diff[i, 0] + diff[i, last]))
                for a in range(1, half):
                    minus = minus + even[a] * float(0.5 * (diff[i, a] + diff[i, last - a]))
                if n % 2:
                    minus = minus + parts[half] * float(diff[i, half])
                zx[i, r : r + 16, c : c + 128] = plus + minus
                zx[last - i, r : r + 16, c : c + 128] = plus - minus

    own_flat = own[...].reshape(6 * ROWS, LANES)[:, :plane]
    own_modes = (
        jnp.dot(own_flat, fwd_ref[0, :, :LANES], preferred_element_type=F32)
        + jnp.dot(own_flat, fwd_ref[1, :, :LANES], preferred_element_type=F32)
    ).reshape(6, ROWS, LANES)

    for copy in copies:
        copy.wait()

    far = jnp.concatenate([remote[...], own[5:6], own[4:5]], axis=0)
    far = far.reshape(6 * ROWS, LANES)[:, :plane]
    far_modes = (
        jnp.dot(far, fwd_ref[0], preferred_element_type=F32)
        + jnp.dot(far, fwd_ref[1], preferred_element_type=F32)
    ).reshape(6, ROWS, 2 * LANES)
    ones = jnp.ones((1, LANES), F32)
    sign_first = lane_ref[4:5, :]
    sign_second = lane_ref[5:6, :]
    modes = []
    for face in range(6):
        code = code_ref[0, face]
        order = order_ref[0, face].astype(F32)
        swap = code >= 4
        rev_a = lax.rem(lax.div(code, 2), 2)
        rev_b = lax.rem(code, 2)
        use_first = jnp.where(swap, rev_b, rev_a) == 1
        use_second = jnp.where(swap, rev_a, rev_b) == 1
        sign = jnp.where(use_first, sign_first, ones) * jnp.where(use_second, sign_second, ones)
        keep = jnp.where((first < order) & (second < order), 1.0, 0.0)
        turned = jnp.where(swap, far_modes[face, :, LANES:], far_modes[face, :, :LANES])
        modes.append((turned * sign - own_modes[face]) * keep)
    modes = jnp.concatenate(modes, axis=0)[:, :plane]
    modes_hi = modes.astype(BF)
    modes_lo = (modes - modes_hi.astype(F32)).astype(BF)
    modes = modes_hi
    jump = (
        jnp.dot(modes_lo, back_ref[0], preferred_element_type=F32)
        + jnp.dot(modes, back_ref[0], preferred_element_type=F32)
        + jnp.dot(modes, back_ref[1], preferred_element_type=F32)
    ).reshape(6, ROWS, LANES)
    lift = 0.5 * last * last * 0.5
    jump = jump * lift

    row_int = lax.broadcasted_iota(jnp.int32, (plane, LANES), 0)
    row_second = row_int - n * lax.div(row_int, n)
    col = lax.broadcasted_iota(jnp.int32, (plane, LANES), 1)
    places = [row_second, row_second + n * last, row_second * n, row_second * n + last]
    blocks = [[], [], [], []]
    for f in range(4):
        for i in range(n):
            blocks[f].append(jnp.where(first == float(i), jump[f + 2], 0.0).astype(BF))
    scat = []
    for axis in range(2):
        total = None
        for side in range(2):
            f = 2 * axis + side
            put = jnp.where(col == places[f], 1.0 if side else -1.0, 0.0).astype(BF)
            part = jnp.dot(
                jnp.concatenate(blocks[f], axis=0)[:, :plane], put, preferred_element_type=F32
            )
            total = part if total is None else total + part
        scat.append(total.reshape(n, ROWS, LANES))

    gain_y = lane_ref[2:3, :] * (TIME_STEP * jac_ref[0, 1])
    gain_z = lane_ref[3:4, :] * (TIME_STEP * jac_ref[0, 2])
    gain_x = TIME_STEP * jac_ref[0, 0]
    zx[0] = zx[0] - jump[0]
    zx[last] = zx[last] + jump[1]

    def keep_both(i, axis, value):
        hi = value.astype(BF)
        zs[i, axis] = hi
        zl[i, axis] = (value - hi.astype(F32)).astype(BF)

    for i in range(n):
        keep_both(i, 0, zx[i])
        keep_both(i, 1, zyz[i, :, :LANES] + scat[0][i])
        keep_both(i, 2, zyz[i, :, LANES:] + scat[1][i])
        both = jnp.dot(
            flux_both, zs[i].reshape(3 * ROWS, LANES), preferred_element_type=F32
        )
        moved = both[:ROWS] + both[ROWS:] + jnp.dot(
            flux_hi, zl[i].reshape(3 * ROWS, LANES), preferred_element_type=F32
        )
        moved = moved + scat[0][i] * gain_y + scat[1][i] * gain_z
        if i == 0:
            moved = moved + jump[0] * gain_x
        if i == last:
            moved = moved + jump[1] * gain_x
        out_ref[:, 0, plane * i : plane * (i + 1)] = moved[:width, :plane]


def solution(mesh):
    sizes = (mesh.shape["blk"], mesh.shape["sub"])

    def on_device(fields, flux_matrix, inv_jacobian, neighbour, orientation, face_order):
        points = fields.shape[2]
        n = round(points ** (1.0 / 3.0))
        deriv, fwd, back, lanes, diff = tables(n)
        smem = pl.BlockSpec(memory_space=pltpu.SMEM)
        vmem = pl.BlockSpec(memory_space=pltpu.VMEM)
        turned = jnp.swapaxes(fields, 0, 1)
        result = pl.pallas_call(
            functools.partial(body, n, diff, sizes),
            out_shape=jax.ShapeDtypeStruct(turned.shape, F32),
            in_specs=[smem] * 3 + [vmem] * 6,
            out_specs=vmem,
            scratch_shapes=[
                pltpu.VMEM((n, ROWS, LANES), F32),
                pltpu.VMEM((n, ROWS, LANES), BF),
                pltpu.VMEM((n, ROWS, LANES), BF),
                pltpu.VMEM((n, 3, ROWS, LANES), BF),
                pltpu.VMEM((n, 3, ROWS, LANES), BF),
                pltpu.VMEM((n, ROWS, 2 * LANES), F32),
                pltpu.VMEM((n, ROWS, LANES), F32),
                pltpu.VMEM((6, ROWS, LANES), BF),
                pltpu.VMEM((4, ROWS, LANES), BF),
                pltpu.VMEM((3, ROWS, ROWS), F32),
                pltpu.SemaphoreType.DMA((4,)),
                pltpu.SemaphoreType.DMA((4,)),
            ],
            compiler_params=pltpu.CompilerParams(
                collective_id=0, has_side_effects=True, vmem_limit_bytes=48 * 1024 * 1024
            ),
        )(
            orientation, face_order, inv_jacobian, turned, flux_matrix,
            jnp.asarray(deriv), jnp.asarray(fwd), jnp.asarray(back), jnp.asarray(lanes),
        )
        return jnp.swapaxes(result, 0, 1)

    return jax.shard_map(
        on_device,
        mesh=mesh,
        in_specs=(
            P(("blk", "sub"), None, None),
            P(),
            P(("blk", "sub"), None),
            P(("blk", "sub"), None),
            P(("blk", "sub"), None),
            P(("blk", "sub"), None),
        ),
        out_specs=P(("blk", "sub"), None, None),
        check_vma=False,
    )
```
